32 devices in a mesh: band: 8 (over z, core), grid: 4 (over y, x).
Axes of the slice: x: 2, y: 2, z: 4, core: 2. Of those that a mesh axis runs over, the one named last changes fastest.
Arguments:
- orbitals: float32 [8, 128, 128, 128], P('band', 'grid')
- sources: int32 [4], replicated, may hold values from 0 to 7, as said below
Outputs:
- compressed: float32 [8, 128, 128, 128], P(None, 'grid', 'band')
The draws below stay inside these ranges and needn't reach their ends.
Inputs may be any that keep to these rules, and one draw needn't show every extreme that they name: `sources`: 4 distinct orbital indices in some order.
All inputs are finite; a program needn't handle non-finite values.
Results may differ from the reference program's by a relative error of at most 0.0003.
Values sent between devices are 32-bit elements; how exact they have to be, the bound alone decides.
A program may use at most 64 MiB of HBM per device.

```python
import math
import jax
import jax.numpy as jnp
from jax import lax

NX = 128
NY = 128
NZ = 128
ROUNDS = 4
NB = 8


def draw_orbitals(key, part):
    first_key, second_key = jax.random.split(jax.random.fold_in(key, 11))
    shape = (NB, NX, NY, NZ)
    rough = jax.random.normal(first_key, shape, jnp.float32)
    spread = 0.15
    coeffs = jax.random.normal(second_key, (NB, 4), jnp.float32) * spread
    xpos = jnp.arange(NX, dtype=jnp.float32)[:, None, None] * (2.0 * math.pi / NX)
    ypos = jnp.arange(NY, dtype=jnp.float32)[None, :, None] * (2.0 * math.pi / NY)
    zpos = jnp.arange(NZ, dtype=jnp.float32)[None, None, :] * (2.0 * math.pi / NZ)
    ones_field = jnp.ones((NX, NY, NZ), jnp.float32)
    modes = jnp.stack([ones_field, jnp.cos(xpos) + 0.0 * ones_field, jnp.cos(ypos) + 0.0 * ones_field, jnp.cos(xpos + zpos) + 0.0 * ones_field])
    smooth = jnp.einsum('bm,mxyz->bxyz', coeffs, modes)
    return rough + smooth


def draw_sources(key, part):
    first_key, second_key = jax.random.split(jax.random.fold_in(key, 7))
    middle = 1 + jax.random.permutation(first_key, NB - 2)
    chosen = jnp.concatenate([jnp.array([0, NB - 1], jnp.int32), middle[:ROUNDS - 2].astype(jnp.int32)])
    chosen = chosen[:ROUNDS]
    order = jax.random.permutation(second_key, ROUNDS)
    return chosen[order].astype(jnp.int32)


def setup_inputs(seed: int = 0) -> dict:
    seeds = jax.random.split(jax.random.key(seed), 3)
    return {
        "orbitals": draw_orbitals(jax.random.fold_in(seeds[2], 71), 0),
        "sources": draw_sources(jax.random.fold_in(seeds[2], 71), 0),
    }


def squared_waves(length):
    index_values = jnp.arange(length, dtype=jnp.int32)
    signed = jnp.where(index_values < length // 2, index_values, index_values - length)
    waves = signed.astype(jnp.float32) * (2.0 * math.pi / length)
    return waves * waves

def reference(orbitals, sources):
    screen = (4.0 * math.pi / NX) ** 2
    waves = squared_waves(NX)[:, None, None] + squared_waves(NY)[None, :, None] + squared_waves(NZ)[None, None, :]
    kernel = 1.0 / (waves + screen)
    picked = orbitals[sources]

    def one_target(target):
        total = jnp.zeros((NX, NY, NZ), jnp.float32)
        for turn in range(ROUNDS):
            source = picked[turn]
            density = target * source
            spectrum = jnp.fft.fftn(density) * kernel
            potential = jnp.real(jnp.fft.ifftn(spectrum)).astype(jnp.float32)
            total = total + source * potential
        return total
    terms = lax.map(one_target, orbitals, batch_size=8)
    flat_orbitals = orbitals.reshape(NB, NX * NY * NZ)
    flat_terms = terms.reshape(NB, NX * NY * NZ)
    volume = 1.0 / (NX * NY * NZ)
    intersection = jnp.dot(flat_orbitals.astype(jnp.float32), flat_terms.T.astype(jnp.float32), precision=lax.Precision.HIGHEST, preferred_element_type=jnp.float32) * volume
    factor = jnp.linalg.cholesky(intersection)
    solved = lax.linalg.triangular_solve(factor, flat_terms, left_side=True, lower=True)
    return (-solved).reshape(NB, NX, NY, NZ)
```

```python
import functools
import math

import jax
import jax.numpy as jnp
import numpy as np
from jax import lax
from jax.experimental import pallas as pl
from jax.experimental.pallas import tpu as pltpu
from jax.sharding import PartitionSpec as P

highest = lax.Precision.HIGHEST
MESH = pl.DeviceIdType.MESH


def spread_2(block, axis, owner):
    block = jnp.where(lax.axis_index(axis) == owner, block, jnp.zeros_like(block))
    return lax.psum(block, axis)


def cas_table(length):
    index_values = jnp.arange(length, dtype=jnp.int32)
    products = index_values[:, None] * index_values[None, :] % length
    angles = products.astype(jnp.float32) * (2.0 * math.pi / length)
    return jnp.cos(angles) + jnp.sin(angles)


def squared_waves(start, count, length):
    index_values = start + jnp.arange(count, dtype=jnp.int32)
    signed = jnp.where(index_values < length // 2, index_values, index_values - length)
    waves = signed.astype(jnp.float32) * (2.0 * math.pi / length)
    return waves * waves


def general(orbitals, sources):
    band_count, slab_x, full_y, full_z = orbitals.shape
    grid_count = lax.axis_size("grid")
    full_x = slab_x * grid_count
    total_bands = band_count * lax.axis_size("band")
    round_count = sources.shape[0]
    table_x = cas_table(full_x)
    table_y = cas_table(full_y)
    table_z = cas_table(full_z)
    column_y = full_y // grid_count
    start_y = lax.axis_index("grid") * column_y
    waves = (
        squared_waves(0, full_x, full_x)[:, None, None]
        + squared_waves(start_y, column_y, full_y)[None, :, None]
        + squared_waves(0, full_z, full_z)[None, None, :]
    )
    screen = (4.0 * math.pi / full_x) ** 2
    volume = 1.0 / (full_x * full_y * full_z)
    kernel = volume / (waves + screen)

    def plane_transform(field):
        spread = jnp.einsum("bxyz,zk->bxyk", field, table_z, precision=highest)
        return jnp.einsum("bxyk,yj->bxjk", spread, table_y, precision=highest)

    def own_slab(number):
        owner = number // band_count
        local = number % band_count
        return (owner, lax.dynamic_index_in_dim(orbitals, local, 0, keepdims=False))

    def fetch(number):
        owner, slab = own_slab(number)
        return spread_2(slab, "band", owner)

    arrived = [fetch(sources[turn]) for turn in range(round_count)]
    terms = jnp.zeros(orbitals.shape, jnp.float32)
    for turn in range(round_count):
        source = arrived[turn][None]
        spectra = plane_transform(orbitals * source)
        potential_columns = lax.all_to_all(spectra, "grid", split_axis=2, concat_axis=1, tiled=True)
        line_spread = jnp.einsum("bxyz,xa->bayz", potential_columns, table_x, precision=highest)
        line_spread = line_spread * kernel[None]
        filtered = jnp.einsum("bayz,ax->bxyz", line_spread, table_x, precision=highest)
        terms = terms + source * plane_transform(
            lax.all_to_all(filtered, "grid", split_axis=1, concat_axis=2, tiled=True)
        )
    orbital_cols, term_cols = (
        lax.all_to_all(orbitals, "band", split_axis=2, concat_axis=0, tiled=True),
        lax.all_to_all(terms, "band", split_axis=2, concat_axis=0, tiled=True),
    )
    flat_orbitals = orbital_cols.reshape(total_bands, -1)
    flat_terms = term_cols.reshape(total_bands, -1)
    partial_intersection = (
        jnp.dot(flat_orbitals, flat_terms.T, precision=highest, preferred_element_type=jnp.float32)
        * volume
    )
    intersection = lax.psum(partial_intersection, ("band", "grid"))
    factor = jnp.linalg.cholesky(intersection)
    solved = lax.linalg.triangular_solve(factor, flat_terms, left_side=True, lower=True)
    return (-solved).reshape(term_cols.shape)


def parts_of(value):
    high = value.astype(jnp.bfloat16)
    low = (value - high.astype(jnp.float32)).astype(jnp.bfloat16)
    return high, low


def along_rows(left, first, second):
    n = first.shape[0]
    h0, l0 = parts_of(first)
    h1, l1 = parts_of(second)
    right = jnp.concatenate(
        [jnp.concatenate([h0, h1], axis=1), jnp.concatenate([l0, l1], axis=1)], axis=0
    )
    both = jnp.dot(left, right, preferred_element_type=jnp.float32)
    return both[:n] + both[n:]


def along_lanes(rows, right):
    n = rows.shape[1]
    high, low = parts_of(rows)
    both = jnp.dot(
        jnp.concatenate([high, low], axis=1), right, preferred_element_type=jnp.float32
    )
    return both[:, :n] + both[:, n:]


def whole_kernel(
    bands, grids, rounds, chunks, n, volume, screen,
    sources, orbitals, left_ref, right_ref, waves_ref, out, *scratch,
):
    gath = scratch[:chunks]
    (spec, cols, back, terms, tcol, part, sums_b, sums_g, splat, in_sem,
     g_recv, up_send, dn_send, pt_send, f_send, f_recv, b_send, b_recv,
     t_send, t_recv, sb_send, sb_recv, sg_send, sg_recv) = scratch[chunks:]
    b = lax.axis_index("band")
    g = lax.axis_index("grid")
    nz = bands // 2
    z, core = b // 2, b % 2
    slab = n // grids
    depth = slab // chunks
    ycols = n // grids
    piece = ycols * depth
    yb = n // bands
    partner = z * 2 + (1 - core)

    barrier = pltpu.get_barrier_semaphore()
    for d in range(1, bands):
        pl.semaphore_signal(barrier, inc=1, device_id=(lax.rem(b + d, bands), g), device_id_type=MESH)
    for d in range(1, grids):
        pl.semaphore_signal(barrier, inc=1, device_id=(b, lax.rem(g + d, grids)), device_id_type=MESH)
    loads = [
        pltpu.make_async_copy(
            orbitals.at[0, pl.ds(c * depth, depth)], gath[c].at[b], in_sem.at[c]
        )
        for c in range(chunks)
    ]
    for load in loads:
        load.start()
    pl.semaphore_wait(barrier, bands + grids - 2)

    def slab_copy(c, origin, target, send):
        return pltpu.make_async_remote_copy(
            src_ref=gath[c].at[origin], dst_ref=gath[c].at[origin],
            send_sem=send, recv_sem=g_recv.at[origin * chunks + c],
            device_id=(target, g), device_id_type=MESH,
        )

    def go_up(c, d):
        return slab_copy(c, (z - d) * 2 + core, (z + 1) * 2 + core, up_send.at[d * chunks + c])

    def go_down(c, d):
        return slab_copy(c, (z + d) * 2 + core, (z - 1) * 2 + core, dn_send.at[d * chunks + c])

    def go_partner(c, zz):
        return slab_copy(c, zz * 2 + core, partner, pt_send.at[zz * chunks + c])

    def own_sends(c):
        loads[c].wait()

        @pl.when(z + 1 < nz)
        def _():
            go_up(c, 0).start()

        @pl.when(z > 0)
        def _():
            go_down(c, 0).start()

        go_partner(c, z).start()

    def arrivals(c):
        for d in range(1, nz):
            @pl.when(z - d >= 0)
            def _():
                slab_copy(c, (z - d) * 2 + core, partner, pt_send.at[0]).wait_recv()

                @pl.when(z + 1 < nz)
                def _():
                    go_up(c, d).start()

                go_partner(c, z - d).start()

            @pl.when(z + d < nz)
            def _():
                slab_copy(c, (z + d) * 2 + core, partner, pt_send.at[0]).wait_recv()

                @pl.when(z > 0)
                def _():
                    go_down(c, d).start()

                go_partner(c, z + d).start()

    def partner_arrivals(c):
        for zz in range(nz):
            slab_copy(c, zz * 2 + (1 - core), partner, pt_send.at[0]).wait_recv()

    left = left_ref[...]
    right = right_ref[...]

    def f_copy(c, r, target, owner):
        return pltpu.make_async_remote_copy(
            src_ref=spec.at[c * rounds + r, pl.ds(target * piece, piece)],
            dst_ref=cols.at[r, owner * chunks + c],
            send_sem=f_send.at[(c * rounds + r) * grids + target],
            recv_sem=f_recv.at[(c * rounds + r) * grids + owner],
            device_id=(b, target), device_id_type=MESH,
        )

    def b_copy(c, r, target, owner):
        return pltpu.make_async_remote_copy(
            src_ref=cols.at[r, target * chunks + c],
            dst_ref=back.at[c * rounds + r, pl.ds(owner * piece, piece)],
            send_sem=b_send.at[(c * rounds + r) * grids + target],
            recv_sem=b_recv.at[(c * rounds + r) * grids + owner],
            device_id=(b, target), device_id_type=MESH,
        )

    own_sends(0)
    for c in range(chunks):
        arrivals(c)
        if c + 1 < chunks:
            own_sends(c + 1)
        partner_arrivals(c)

        def forward(r, _, c=c):
            s = sources[r]
            for k in range(0, depth, 2):
                pair = gath[c][s, pl.ds(k, 2)] * gath[c][b, pl.ds(k, 2)]
                rows = along_lanes(pair.reshape(2 * n, n), right)
                planes = along_rows(left, rows[:n], rows[n:])
                spec[c * rounds + r, pl.ds(k, n, stride=depth), :] = planes[:, :n]
                spec[c * rounds + r, pl.ds(k + 1, n, stride=depth), :] = planes[:, n:]
            for d in range(1, grids):
                f_copy(c, r, lax.rem(g + d, grids), g).start()
            cols[r, g * chunks + c] = spec[c * rounds + r, pl.ds(g * piece, piece), :]
            return 0

        lax.fori_loop(0, rounds, forward, 0)

    base = waves_ref[...]
    for r in range(rounds):
        for c in range(chunks):
            for d in range(1, grids):
                f_copy(c, r, g, lax.rem(g + d, grids)).wait_recv()

        def line(k, _, r=r):
            lines = [
                cols[r, :, pl.ds(pl.multiple_of((2 * k + e) * depth, depth), depth), :].reshape(n, n)
                for e in range(2)
            ]
            moved = along_rows(left, lines[0], lines[1])
            filtered = []
            for e in range(2):
                ky = g * ycols + 2 * k + e
                signed = jnp.where(ky < n // 2, ky, ky - n).astype(jnp.float32)
                wave = signed * (2.0 * math.pi / n)
                filtered.append(moved[:, e * n:(e + 1) * n] * (volume / (base + wave * wave)))
            done = along_rows(left, filtered[0], filtered[1])
            for e in range(2):
                cols[r, :, pl.ds(pl.multiple_of((2 * k + e) * depth, depth), depth), :] = (
                    done[:, e * n:(e + 1) * n].reshape(grids * chunks, depth, n)
                )
            return 0

        lax.fori_loop(0, ycols // 2, line, 0)
        for d in range(1, grids):
            b_copy(0, r, lax.rem(g + d, grids), g).start()
    for c in range(1, chunks):
        for r in range(rounds):
            for d in range(1, grids):
                b_copy(c, r, lax.rem(g + d, grids), g).start()

    def t_copy(c, target, owner):
        return pltpu.make_async_remote_copy(
            src_ref=terms.at[pl.ds(c * depth, depth), pl.ds(target * yb, yb)],
            dst_ref=tcol.at[owner, pl.ds(c * depth, depth)],
            send_sem=t_send.at[c * bands + target],
            recv_sem=t_recv.at[c * bands + owner],
            device_id=(target, g), device_id_type=MESH,
        )

    def overlap(c):
        for d in range(1, bands):
            t_copy(c, b, lax.rem(b + d, bands)).wait_recv()

        def one(i, _):
            mine = gath[c][i, :, pl.ds(b * yb, yb), :]
            for k in range(bands):
                prod = mine * tcol[k, pl.ds(c * depth, depth)]
                total = jnp.sum(prod.reshape(-1, 8, n), axis=0)
                if c == 0:
                    part[i * bands + k] = total
                else:
                    part[i * bands + k] += total
            return 0

        lax.fori_loop(0, bands, one, 0)

    for c in range(chunks):
        for r in range(rounds):
            for d in range(1, grids):
                b_copy(c, r, g, lax.rem(g + d, grids)).wait_recv()
            back[c * rounds + r, pl.ds(g * piece, piece), :] = cols[r, g * chunks + c]
            s = sources[r]

            def inverse(k, _, c=c, r=r, s=s):
                planes = along_rows(
                    left,
                    back[c * rounds + r, pl.ds(2 * k, n, stride=depth), :],
                    back[c * rounds + r, pl.ds(2 * k + 1, n, stride=depth), :],
                )
                rows = jnp.concatenate([planes[:, :n], planes[:, n:]], axis=0)
                potential = along_lanes(rows, right).reshape(2, n, n)
                here = gath[c][s, pl.ds(2 * k, 2)] * potential
                if r == 0:
                    terms[pl.ds(c * depth + 2 * k, 2)] = here
                else:
                    terms[pl.ds(c * depth + 2 * k, 2)] += here
                return 0

            for k in range(depth // 2):
                inverse(k, 0)
        for d in range(1, bands):
            t_copy(c, lax.rem(b + d, bands), b).start()
        tcol[b, pl.ds(c * depth, depth)] = terms[pl.ds(c * depth, depth), pl.ds(b * yb, yb), :]
        if c > 0:
            overlap(c - 1)
    overlap(chunks - 1)

    count = bands * bands
    flat = jnp.sum(part[...], axis=1)
    if count < n:
        flat = jnp.concatenate([flat, jnp.zeros((n - count, n), jnp.float32)], axis=0)
    lanes = jnp.sum(flat.T, axis=0, keepdims=True)
    sums_b[b] = jnp.broadcast_to(lanes, (8, n))

    def sb_copy(target, owner):
        return pltpu.make_async_remote_copy(
            src_ref=sums_b.at[b], dst_ref=sums_b.at[owner],
            send_sem=sb_send.at[target], recv_sem=sb_recv.at[owner],
            device_id=(target, g), device_id_type=MESH,
        )

    def sg_copy(target, owner):
        return pltpu.make_async_remote_copy(
            src_ref=sums_g.at[g], dst_ref=sums_g.at[owner],
            send_sem=sg_send.at[target], recv_sem=sg_recv.at[owner],
            device_id=(b, target), device_id_type=MESH,
        )

    for d in range(1, bands):
        sb_copy(lax.rem(b + d, bands), b).start()
    for d in range(1, bands):
        sb_copy(b, lax.rem(b + d, bands)).wait_recv()
    sums_g[g] = jnp.sum(sums_b[...], axis=0)
    for d in range(1, grids):
        sg_copy(lax.rem(g + d, grids), g).start()
    for d in range(1, grids):
        sg_copy(g, lax.rem(g + d, grids)).wait_recv()
    total = jnp.sum(sums_g[...], axis=0)[:1] * volume
    splat[...] = jnp.broadcast_to(total, (n, n)).T

    def entry(i, k):
        first = splat[pl.ds(i * bands + k, 1), :]
        return 0.5 * (first + splat[pl.ds(k * bands + i, 1), :])

    factor = {}
    inverse_diag = {}
    for k in range(bands):
        diag = entry(k, k)
        for m in range(k):
            diag = diag - factor[k, m] * factor[k, m]
        inverse_diag[k] = 1.0 / jnp.sqrt(diag)
        for i in range(k + 1, bands):
            value = entry(i, k)
            for m in range(k):
                value = value - factor[i, m] * factor[k, m]
            factor[i, k] = value * inverse_diag[k]
    for k in range(bands):
        splat[pl.ds(k * bands + k, 1), :] = inverse_diag[k]
        for i in range(k + 1, bands):
            splat[pl.ds(i * bands + k, 1), :] = factor[i, k]

    def solve(x, _):
        solved = []
        for i in range(bands):
            value = -tcol[i, x]
            for k in range(i):
                value = value - splat[pl.ds(i * bands + k, 1), :] * solved[k]
            value = value * splat[pl.ds(i * bands + i, 1), :]
            out[i, x] = value
            solved.append(value)
        return 0

    lax.fori_loop(0, slab, solve, 0)

    for c in range(chunks):
        for d in range(nz):
            @pl.when(jnp.logical_and(z - d >= 0, z + 1 < nz))
            def _():
                go_up(c, d).wait_send()

            @pl.when(jnp.logical_and(z + d < nz, z > 0))
            def _():
                go_down(c, d).wait_send()

            go_partner(c, d).wait_send()
        for r in range(rounds):
            for d in range(1, grids):
                f_copy(c, r, lax.rem(g + d, grids), g).wait_send()
                b_copy(c, r, lax.rem(g + d, grids), g).wait_send()
        for d in range(1, bands):
            t_copy(c, lax.rem(b + d, bands), b).wait_send()
    for d in range(1, bands):
        sb_copy(lax.rem(b + d, bands), b).wait_send()
    for d in range(1, grids):
        sg_copy(lax.rem(g + d, grids), g).wait_send()


def fused(bands, grids, orbitals, sources):
    n = orbitals.shape[2]
    rounds = sources.shape[0]
    slab = n // grids
    depth = 8
    chunks = slab // depth
    yb = n // bands
    numbers = np.arange(n)
    angles = (numbers[:, None] * numbers[None, :] % n) * (2.0 * math.pi / n)
    table = jnp.asarray(np.cos(angles) + np.sin(angles), jnp.float32)
    high, low = parts_of(table)
    left = jnp.block([[high, high], [low, low]])
    right = jnp.block([[high, low], [high, low]])
    signed = np.where(numbers < n // 2, numbers, numbers - n) * (2.0 * math.pi / n)
    screen = (4.0 * math.pi / n) ** 2
    waves = jnp.asarray(signed[:, None] ** 2 + signed[None, :] ** 2 + screen, jnp.float32)
    volume = 1.0 / n**3
    f32 = jnp.float32
    dma = pltpu.SemaphoreType.DMA
    scratch = [pltpu.VMEM((bands, depth, n, n), f32) for _ in range(chunks)]
    scratch += [
        pltpu.VMEM((chunks * rounds, n * depth, n), f32),
        pltpu.VMEM((rounds, grids * chunks, (n // grids) * depth, n), f32),
        pltpu.VMEM((chunks * rounds, n * depth, n), f32),
        pltpu.VMEM((slab, n, n), f32),
        pltpu.VMEM((bands, slab, yb, n), f32),
        pltpu.VMEM((bands * bands, 8, n), f32),
        pltpu.VMEM((bands, 8, n), f32),
        pltpu.VMEM((grids, 8, n), f32),
        pltpu.VMEM((n, n), f32),
        dma((chunks,)),
        dma((bands * chunks,)),
        dma((bands * chunks,)),
        dma((bands * chunks,)),
        dma((bands * chunks,)),
        dma((chunks * rounds * grids,)),
        dma((chunks * rounds * grids,)),
        dma((chunks * rounds * grids,)),
        dma((chunks * rounds * grids,)),
        dma((chunks * bands,)),
        dma((chunks * bands,)),
        dma((bands,)),
        dma((bands,)),
        dma((grids,)),
        dma((grids,)),
    ]
    vmem = pl.BlockSpec(memory_space=pltpu.VMEM)
    return pl.pallas_call(
        functools.partial(whole_kernel, bands, grids, rounds, chunks, n, volume, screen),
        out_shape=jax.ShapeDtypeStruct((bands, slab, yb, n), f32),
        in_specs=[
            pl.BlockSpec(memory_space=pltpu.SMEM),
            pl.BlockSpec(memory_space=pl.ANY),
            vmem, vmem, vmem,
        ],
        out_specs=vmem,
        scratch_shapes=scratch,
        compiler_params=pltpu.CompilerParams(
            collective_id=0, has_side_effects=True, vmem_limit_bytes=60 * 1024 * 1024
        ),
        name="exchange",
    )(sources, orbitals, left, right, waves)


def per_device(orbitals, sources):
    held, slab, full_y, full_z = orbitals.shape
    bands = lax.axis_size("band")
    grids = lax.axis_size("grid")
    n = full_y
    fits = (
        held == 1 and n == full_z == slab * grids and n % 128 == 0 and slab % 8 == 0
        and bands % 2 == 0 and bands * bands <= n and n % (8 * bands) == 0
        and 4 * n * n * slab * (bands + 3 * sources.shape[0] + 3) <= 50 * 2**20
    )
    if fits:
        return fused(bands, grids, orbitals, sources)
    return general(orbitals, sources)


def solution(mesh):
    placed = (P("band", "grid", None, None), P())
    return jax.shard_map(
        per_device,
        mesh=mesh,
        in_specs=placed,
        out_specs=P(None, "grid", "band", None),
        check_vma=False,
    )
```

```python
import functools
import math

import jax
import jax.numpy as jnp
import numpy as np
from jax import lax
from jax.experimental import pallas as pl
from jax.experimental.pallas import tpu as pltpu
from jax.sharding import PartitionSpec as P

highest = lax.Precision.HIGHEST
MESH = pl.DeviceIdType.MESH


def spread_2(block, axis, owner):
    block = jnp.where(lax.axis_index(axis) == owner, block, jnp.zeros_like(block))
    return lax.psum(block, axis)


def cas_table(length):
    index_values = jnp.arange(length, dtype=jnp.int32)
    products = index_values[:, None] * index_values[None, :] % length
    angles = products.astype(jnp.float32) * (2.0 * math.pi / length)
    return jnp.cos(angles) + jnp.sin(angles)


def squared_waves(start, count, length):
    index_values = start + jnp.arange(count, dtype=jnp.int32)
    signed = jnp.where(index_values < length // 2, index_values, index_values - length)
    waves = signed.astype(jnp.float32) * (2.0 * math.pi / length)
    return waves * waves


def general(orbitals, sources):
    band_count, slab_x, full_y, full_z = orbitals.shape
    grid_count = lax.axis_size("grid")
    full_x = slab_x * grid_count
    total_bands = band_count * lax.axis_size("band")
    round_count = sources.shape[0]
    table_x = cas_table(full_x)
    table_y = cas_table(full_y)
    table_z = cas_table(full_z)
    column_y = full_y // grid_count
    start_y = lax.axis_index("grid") * column_y
    waves = (
        squared_waves(0, full_x, full_x)[:, None, None]
        + squared_waves(start_y, column_y, full_y)[None, :, None]
        + squared_waves(0, full_z, full_z)[None, None, :]
    )
    screen = (4.0 * math.pi / full_x) ** 2
    volume = 1.0 / (full_x * full_y * full_z)
    kernel = volume / (waves + screen)

    def plane_transform(field):
        spread = jnp.einsum("bxyz,zk->bxyk", field, table_z, precision=highest)
        return jnp.einsum("bxyk,yj->bxjk", spread, table_y, precision=highest)

    def own_slab(number):
        owner = number // band_count
        local = number % band_count
        return (owner, lax.dynamic_index_in_dim(orbitals, local, 0, keepdims=False))

    def fetch(number):
        owner, slab = own_slab(number)
        return spread_2(slab, "band", owner)

    arrived = [fetch(sources[turn]) for turn in range(round_count)]
    terms = jnp.zeros(orbitals.shape, jnp.float32)
    for turn in range(round_count):
        source = arrived[turn][None]
        spectra = plane_transform(orbitals * source)
        potential_columns = lax.all_to_all(spectra, "grid", split_axis=2, concat_axis=1, tiled=True)
        line_spread = jnp.einsum("bxyz,xa->bayz", potential_columns, table_x, precision=highest)
        line_spread = line_spread * kernel[None]
        filtered = jnp.einsum("bayz,ax->bxyz", line_spread, table_x, precision=highest)
        terms = terms + source * plane_transform(
            lax.all_to_all(filtered, "grid", split_axis=1, concat_axis=2, tiled=True)
        )
    orbital_cols, term_cols = (
        lax.all_to_all(orbitals, "band", split_axis=2, concat_axis=0, tiled=True),
        lax.all_to_all(terms, "band", split_axis=2, concat_axis=0, tiled=True),
    )
    flat_orbitals = orbital_cols.reshape(total_bands, -1)
    flat_terms = term_cols.reshape(total_bands, -1)
    partial_intersection = (
        jnp.dot(flat_orbitals, flat_terms.T, precision=highest, preferred_element_type=jnp.float32)
        * volume
    )
    intersection = lax.psum(partial_intersection, ("band", "grid"))
    factor = jnp.linalg.cholesky(intersection)
    solved = lax.linalg.triangular_solve(factor, flat_terms, left_side=True, lower=True)
    return (-solved).reshape(term_cols.shape)


def parts_of(value):
    high = value.astype(jnp.bfloat16)
    low = (value - high.astype(jnp.float32)).astype(jnp.bfloat16)
    return high, low


def along_rows(left, first, second):
    n = first.shape[0]
    h0, l0 = parts_of(first)
    h1, l1 = parts_of(second)
    right = jnp.concatenate(
        [jnp.concatenate([h0, h1], axis=1), jnp.concatenate([l0, l1], axis=1)], axis=0
    )
    both = jnp.dot(left, right, preferred_element_type=jnp.float32)
    return both[:n] + both[n:]


def along_lanes(rows, right):
    n = rows.shape[1]
    high, low = parts_of(rows)
    both = jnp.dot(
        jnp.concatenate([high, low], axis=1), right, preferred_element_type=jnp.float32
    )
    return both[:, :n] + both[:, n:]


def whole_kernel(
    bands, grids, rounds, chunks, unit, n, volume,
    sources, orbitals, left_ref, right_ref, waves_ref, out, *scratch,
):
    (own, mate, up, dn, src, fcol, spec, cols, back, terms, tcol, part, sums_b, sums_g, splat,
     in_sem, m_send, m_recv, up_send, up_recv, dn_send, dn_recv, s_send, s_recv,
     o_send, o_recv, f_send, f_recv, b_send, b_recv,
     t_send, t_recv, sb_send, sb_recv, sg_send, sg_recv) = scratch
    b = lax.axis_index("band")
    g = lax.axis_index("grid")
    nz = bands // 2
    z, core = b // 2, b % 2
    slab = n // grids
    depth = slab // chunks
    ycols = n // grids
    piece = ycols * depth
    yb = n // bands
    half = slab // 2
    units = half // unit
    total_units = rounds * units
    partner = z * 2 + (1 - core)

    barrier = pltpu.get_barrier_semaphore()
    for d in range(1, bands):
        pl.semaphore_signal(barrier, inc=1, device_id=(lax.rem(b + d, bands), g), device_id_type=MESH)
    for d in range(1, grids):
        pl.semaphore_signal(barrier, inc=1, device_id=(b, lax.rem(g + d, grids)), device_id_type=MESH)
    loads = [
        pltpu.make_async_copy(
            orbitals.at[0, pl.ds(h * half, half)], own.at[pl.ds(h * half, half)], in_sem.at[h]
        )
        for h in range(2)
    ]
    for load in loads:
        load.start()
    for load in loads:
        load.wait()
    pl.semaphore_wait(barrier, bands + grids - 2)

    def mate_copy(u):
        return pltpu.make_async_remote_copy(
            src_ref=own.at[pl.ds((1 - core) * half + u * unit, unit)],
            dst_ref=mate.at[pl.ds(u * unit, unit)],
            send_sem=m_send.at[u], recv_sem=m_recv.at[u],
            device_id=(partner, g), device_id_type=MESH,
        )

    def up_copy(v):
        return pltpu.make_async_remote_copy(
            src_ref=up.at[v], dst_ref=up.at[v],
            send_sem=up_send.at[v], recv_sem=up_recv.at[v],
            device_id=(lax.rem(b + 2, bands), g), device_id_type=MESH,
        )

    def dn_copy(v):
        return pltpu.make_async_remote_copy(
            src_ref=dn.at[v], dst_ref=dn.at[v],
            send_sem=dn_send.at[v], recv_sem=dn_recv.at[v],
            device_id=(lax.rem(b + bands - 2, bands), g), device_id_type=MESH,
        )

    def src_copy(v, side):
        r, u = lax.div(v, units), lax.rem(v, units)
        block = src.at[r, pl.ds(side * half + u * unit, unit)]
        return pltpu.make_async_remote_copy(
            src_ref=block, dst_ref=block,
            send_sem=s_send.at[v], recv_sem=s_recv.at[v],
            device_id=(partner, g), device_id_type=MESH,
        )

    for u in range(units):
        mate_copy(u).start()

    def step(t, _):
        @pl.when(t < units)
        def _():
            mate_copy(t).wait_recv()

        def pass_on(v, box, copy, first, last):
            @pl.when(jnp.logical_and(v >= 0, v < total_units))
            def _():
                r, u = lax.div(v, units), lax.rem(v, units)
                s = sources[r]
                here = jnp.where(
                    s == b, own[pl.ds(core * half + u * unit, unit)], mate[pl.ds(u * unit, unit)]
                )

                @pl.when(first)
                def _():
                    box[v] = here

                @pl.when(jnp.logical_not(first))
                def _():
                    copy(v).wait_recv()
                    box[v] = jnp.where(jnp.logical_or(s == b, s == partner), here, box[v])

                @pl.when(jnp.logical_not(last))
                def _():
                    copy(v).start()

        pass_on(t - z, up, up_copy, z == 0, z == nz - 1)
        pass_on(t - (nz - 1 - z), dn, dn_copy, z == nz - 1, z == 0)
        v = t - (nz - 1)

        @pl.when(v >= 0)
        def _():
            r, u = lax.div(v, units), lax.rem(v, units)
            src[r, pl.ds(core * half + u * unit, unit)] = jnp.where(
                sources[r] < 2 * z + 2, up[v], dn[v]
            )
            src_copy(v, core).start()

        return 0

    def o_copy(target, owner):
        return pltpu.make_async_remote_copy(
            src_ref=own.at[:, pl.ds(target * yb, yb)], dst_ref=fcol.at[owner],
            send_sem=o_send.at[target], recv_sem=o_recv.at[owner],
            device_id=(target, g), device_id_type=MESH,
        )

    left = left_ref[...]
    right = right_ref[...]

    def f_copy(c, r, target, owner):
        return pltpu.make_async_remote_copy(
            src_ref=spec.at[c * rounds + r, pl.ds(target * piece, piece)],
            dst_ref=cols.at[r, owner * chunks + c],
            send_sem=f_send.at[(c * rounds + r) * grids + target],
            recv_sem=f_recv.at[(c * rounds + r) * grids + owner],
            device_id=(b, target), device_id_type=MESH,
        )

    def b_copy(c, r, target, owner):
        return pltpu.make_async_remote_copy(
            src_ref=cols.at[r, target * chunks + c],
            dst_ref=back.at[c * rounds + r, pl.ds(owner * piece, piece)],
            send_sem=b_send.at[(c * rounds + r) * grids + target],
            recv_sem=b_recv.at[(c * rounds + r) * grids + owner],
            device_id=(b, target), device_id_type=MESH,
        )

    base = waves_ref[...]
    chunk_units = depth // unit

    def forward_chunk(c, r):
        for k in range(0, depth, 2):
            at = c * depth + k
            pair = src[r, pl.ds(at, 2)] * own[pl.ds(at, 2)]
            rows = along_lanes(pair.reshape(2 * n, n), right)
            planes = along_rows(left, rows[:n], rows[n:])
            spec[c * rounds + r, pl.ds(k, n, stride=depth), :] = planes[:, :n]
            spec[c * rounds + r, pl.ds(k + 1, n, stride=depth), :] = planes[:, n:]
        for d in range(1, grids):
            f_copy(c, r, lax.rem(g + d, grids), g).start()
        cols[r, g * chunks + c] = spec[c * rounds + r, pl.ds(g * piece, piece), :]

    def forward(r):
        def phase(i, _):
            start = r * units + i * chunk_units + (nz - 1)
            if r == 0:
                lax.fori_loop(jnp.where(i == 0, 0, start), start + chunk_units, step, 0)
            else:
                lax.fori_loop(start, start + chunk_units, step, 0)

            def side(e, _):
                @pl.when(e == 1)
                def _():
                    for u in range(chunk_units):
                        src_copy(r * units + i * chunk_units + u, 1 - core).wait_recv()

                where = jnp.where(e == 0, core, 1 - core)
                forward_chunk(where * (chunks // 2) + i, r)
                return 0

            lax.fori_loop(0, 2, side, 0)
            return 0

        lax.fori_loop(0, chunks // 2, phase, 0)

    def lines(r):
        for c in range(chunks):
            for d in range(1, grids):
                f_copy(c, r, g, lax.rem(g + d, grids)).wait_recv()

        def line(k, _):
            held = [
                cols[r, :, pl.ds(pl.multiple_of((2 * k + e) * depth, depth), depth), :].reshape(n, n)
                for e in range(2)
            ]
            moved = along_rows(left, held[0], held[1])
            filtered = []
            for e in range(2):
                ky = g * ycols + 2 * k + e
                signed = jnp.where(ky < n // 2, ky, ky - n).astype(jnp.float32)
                wave = signed * (2.0 * math.pi / n)
                filtered.append(moved[:, e * n:(e + 1) * n] * (volume / (base + wave * wave)))
            done = along_rows(left, filtered[0], filtered[1])
            for e in range(2):
                cols[r, :, pl.ds(pl.multiple_of((2 * k + e) * depth, depth), depth), :] = (
                    done[:, e * n:(e + 1) * n].reshape(grids * chunks, depth, n)
                )
            return 0

        lax.fori_loop(0, ycols // 2, line, 0)

    def give_back(c, r):
        for d in range(1, grids):
            b_copy(c, r, lax.rem(g + d, grids), g).start()

    def inverse(c, r):
        for d in range(1, grids):
            b_copy(c, r, g, lax.rem(g + d, grids)).wait_recv()
        back[c * rounds + r, pl.ds(g * piece, piece), :] = cols[r, g * chunks + c]
        for k in range(0, depth, 2):
            planes = along_rows(
                left,
                back[c * rounds + r, pl.ds(k, n, stride=depth), :],
                back[c * rounds + r, pl.ds(k + 1, n, stride=depth), :],
            )
            rows = jnp.concatenate([planes[:, :n], planes[:, n:]], axis=0)
            potential = along_lanes(rows, right).reshape(2, n, n)
            at = c * depth + k
            here = src[r, pl.ds(at, 2)] * potential
            if r == 0:
                terms[pl.ds(at, 2)] = here
            else:
                terms[pl.ds(at, 2)] += here

    def inverse_all(r):
        def one(c, _):
            inverse(c, r)
            return 0

        lax.fori_loop(0, chunks, one, 0)

    tail = min(2, rounds)
    returned = 0
    for r in range(rounds):
        forward(r)
        if r == rounds - 1:
            for d in range(1, bands):
                o_copy(lax.rem(b + d, bands), b).start()
        if r % 2 == 1 and returned < rounds - tail:
            lines(returned)
            for c in range(chunks):
                give_back(c, returned)
            returned += 1
            ready = returned - 1
            if ready > 0:
                inverse_all(ready - 1)
    while returned < rounds - tail:
        lines(returned)
        for c in range(chunks):
            give_back(c, returned)
        returned += 1
        if returned > 1:
            inverse_all(returned - 2)
    for r in range(rounds - tail, rounds):
        lines(r)
    for c in range(chunks):
        for r in range(rounds - tail, rounds):
            give_back(c, r)
    fcol[b] = own[:, pl.ds(b * yb, yb), :]
    if rounds > tail:
        inverse_all(rounds - tail - 1)

    def t_copy(c, target, owner):
        return pltpu.make_async_remote_copy(
            src_ref=terms.at[pl.ds(c * depth, depth), pl.ds(target * yb, yb)],
            dst_ref=tcol.at[owner, pl.ds(c * depth, depth)],
            send_sem=t_send.at[c * bands + target],
            recv_sem=t_recv.at[c * bands + owner],
            device_id=(target, g), device_id_type=MESH,
        )

    def overlap(c):
        for d in range(1, bands):
            t_copy(c, b, lax.rem(b + d, bands)).wait_recv()

        def one(i, _):
            mine = fcol[i, pl.ds(c * depth, depth)]
            for k in range(bands):
                prod = mine * tcol[k, pl.ds(c * depth, depth)]
                total = jnp.sum(prod.reshape(-1, 8, n), axis=0)
                if c == 0:
                    part[i * bands + k] = total
                else:
                    part[i * bands + k] += total
            return 0

        lax.fori_loop(0, bands, one, 0)

    for c in range(chunks):
        for r in range(rounds - tail, rounds):
            inverse(c, r)
        for d in range(1, bands):
            t_copy(c, lax.rem(b + d, bands), b).start()
        tcol[b, pl.ds(c * depth, depth)] = terms[pl.ds(c * depth, depth), pl.ds(b * yb, yb), :]
        if c == 1:
            for d in range(1, bands):
                o_copy(b, lax.rem(b + d, bands)).wait_recv()
        if c > 0:
            overlap(c - 1)
    overlap(chunks - 1)

    count = bands * bands
    flat = jnp.sum(part[...], axis=1)
    if count < n:
        flat = jnp.concatenate([flat, jnp.zeros((n - count, n), jnp.float32)], axis=0)
    lanes = jnp.sum(flat.T, axis=0, keepdims=True)
    sums_b[b] = jnp.broadcast_to(lanes, (8, n))

    def sb_copy(target, owner):
        return pltpu.make_async_remote_copy(
            src_ref=sums_b.at[b], dst_ref=sums_b.at[owner],
            send_sem=sb_send.at[target], recv_sem=sb_recv.at[owner],
            device_id=(target, g), device_id_type=MESH,
        )

    def sg_copy(target, owner):
        return pltpu.make_async_remote_copy(
            src_ref=sums_g.at[g], dst_ref=sums_g.at[owner],
            send_sem=sg_send.at[target], recv_sem=sg_recv.at[owner],
            device_id=(b, target), device_id_type=MESH,
        )

    for d in range(1, bands):
        sb_copy(lax.rem(b + d, bands), b).start()
    for d in range(1, bands):
        sb_copy(b, lax.rem(b + d, bands)).wait_recv()
    sums_g[g] = jnp.sum(sums_b[...], axis=0)
    for d in range(1, grids):
        sg_copy(lax.rem(g + d, grids), g).start()
    for d in range(1, grids):
        sg_copy(g, lax.rem(g + d, grids)).wait_recv()
    total = jnp.sum(sums_g[...], axis=0)[:1] * volume
    splat[...] = jnp.broadcast_to(total, (n, n)).T

    def entry(i, k):
        first = splat[pl.ds(i * bands + k, 1), :]
        return 0.5 * (first + splat[pl.ds(k * bands + i, 1), :])

    factor = {}
    inverse_diag = {}
    for k in range(bands):
        diag = entry(k, k)
        for m in range(k):
            diag = diag - factor[k, m] * factor[k, m]
        inverse_diag[k] = 1.0 / jnp.sqrt(diag)
        for i in range(k + 1, bands):
            value = entry(i, k)
            for m in range(k):
                value = value - factor[i, m] * factor[k, m]
            factor[i, k] = value * inverse_diag[k]
    for k in range(bands):
        splat[pl.ds(k * bands + k, 1), :] = inverse_diag[k]
        for i in range(k + 1, bands):
            splat[pl.ds(i * bands + k, 1), :] = factor[i, k]

    def solve(x, _):
        solved = []
        for i in range(bands):
            value = -tcol[i, x]
            for k in range(i):
                value = value - splat[pl.ds(i * bands + k, 1), :] * solved[k]
            value = value * splat[pl.ds(i * bands + i, 1), :]
            out[i, x] = value
            solved.append(value)
        return 0

    lax.fori_loop(0, slab, solve, 0)

    for u in range(units):
        mate_copy(u).wait_send()

    def settle(v, _):
        @pl.when(z < nz - 1)
        def _():
            up_copy(v).wait_send()

        @pl.when(z > 0)
        def _():
            dn_copy(v).wait_send()

        src_copy(v, core).wait_send()
        return 0

    lax.fori_loop(0, total_units, settle, 0)
    for d in range(1, bands):
        o_copy(lax.rem(b + d, bands), b).wait_send()
    for c in range(chunks):
        for r in range(rounds):
            for d in range(1, grids):
                f_copy(c, r, lax.rem(g + d, grids), g).wait_send()
                b_copy(c, r, lax.rem(g + d, grids), g).wait_send()
        for d in range(1, bands):
            t_copy(c, lax.rem(b + d, bands), b).wait_send()
    for d in range(1, bands):
        sb_copy(lax.rem(b + d, bands), b).wait_send()
    for d in range(1, grids):
        sg_copy(lax.rem(g + d, grids), g).wait_send()


def fused(bands, grids, orbitals, sources):
    n = orbitals.shape[2]
    rounds = sources.shape[0]
    slab = n // grids
    depth = 8
    chunks = slab // depth
    yb = n // bands
    numbers = np.arange(n)
    angles = (numbers[:, None] * numbers[None, :] % n) * (2.0 * math.pi / n)
    table = jnp.asarray(np.cos(angles) + np.sin(angles), jnp.float32)
    high, low = parts_of(table)
    left = jnp.block([[high, high], [low, low]])
    right = jnp.block([[high, low], [high, low]])
    signed = np.where(numbers < n // 2, numbers, numbers - n) * (2.0 * math.pi / n)
    screen = (4.0 * math.pi / n) ** 2
    waves = jnp.asarray(signed[:, None] ** 2 + signed[None, :] ** 2 + screen, jnp.float32)
    volume = 1.0 / n**3
    f32 = jnp.float32
    dma = pltpu.SemaphoreType.DMA
    unit = 2
    units = slab // 2 // unit
    relay = rounds * units
    scratch = [
        pltpu.VMEM((slab, n, n), f32),
        pltpu.VMEM((slab // 2, n, n), f32),
        pltpu.VMEM((relay, unit, n, n), f32),
        pltpu.VMEM((relay, unit, n, n), f32),
        pltpu.VMEM((rounds, slab, n, n), f32),
        pltpu.VMEM((bands, slab, yb, n), f32),
        pltpu.VMEM((chunks * rounds, n * depth, n), f32),
        pltpu.VMEM((rounds, grids * chunks, (n // grids) * depth, n), f32),
        pltpu.VMEM((chunks * rounds, n * depth, n), f32),
        pltpu.VMEM((slab, n, n), f32),
        pltpu.VMEM((bands, slab, yb, n), f32),
        pltpu.VMEM((bands * bands, 8, n), f32),
        pltpu.VMEM((bands, 8, n), f32),
        pltpu.VMEM((grids, 8, n), f32),
        pltpu.VMEM((n, n), f32),
        dma((2,)),
        dma((units,)),
        dma((units,)),
        dma((relay,)),
        dma((relay,)),
        dma((relay,)),
        dma((relay,)),
        dma((relay,)),
        dma((relay,)),
        dma((bands,)),
        dma((bands,)),
        dma((chunks * rounds * grids,)),
        dma((chunks * rounds * grids,)),
        dma((chunks * rounds * grids,)),
        dma((chunks * rounds * grids,)),
        dma((chunks * bands,)),
        dma((chunks * bands,)),
        dma((bands,)),
        dma((bands,)),
        dma((grids,)),
        dma((grids,)),
    ]
    vmem = pl.BlockSpec(memory_space=pltpu.VMEM)
    return pl.pallas_call(
        functools.partial(whole_kernel, bands, grids, rounds, chunks, unit, n, volume),
        out_shape=jax.ShapeDtypeStruct((bands, slab, yb, n), f32),
        in_specs=[
            pl.BlockSpec(memory_space=pltpu.SMEM),
            pl.BlockSpec(memory_space=pl.ANY),
            vmem, vmem, vmem,
        ],
        out_specs=vmem,
        scratch_shapes=scratch,
        compiler_params=pltpu.CompilerParams(
            collective_id=0, has_side_effects=True, vmem_limit_bytes=60 * 1024 * 1024
        ),
        name="exchange",
    )(sources, orbitals, left, right, waves)


def per_device(orbitals, sources):
    held, slab, full_y, full_z = orbitals.shape
    bands = lax.axis_size("band")
    grids = lax.axis_size("grid")
    n = full_y
    fits = (
        held == 1 and n == full_z == slab * grids and n % 128 == 0 and slab % 16 == 0
        and bands % 2 == 0 and bands * bands <= n and n % (8 * bands) == 0
        and 4 * n * n * slab * (5 * sources.shape[0] + 6) <= 54 * 2**20
    )
    if fits:
        return fused(bands, grids, orbitals, sources)
    return general(orbitals, sources)


def solution(mesh):
    placed = (P("band", "grid", None, None), P())
    return jax.shard_map(
        per_device,
        mesh=mesh,
        in_specs=placed,
        out_specs=P(None, "grid", "band", None),
        check_vma=False,
    )
```

```python
import functools
import math

import jax
import jax.numpy as jnp
import numpy as np
from jax import lax
from jax.experimental import pallas as pl
from jax.experimental.pallas import tpu as pltpu
from jax.sharding import PartitionSpec as P

highest = lax.Precision.HIGHEST
MESH = pl.DeviceIdType.MESH


def spread_2(block, axis, owner):
    block = jnp.where(lax.axis_index(axis) == owner, block, jnp.zeros_like(block))
    return lax.psum(block, axis)


def cas_table(length):
    index_values = jnp.arange(length, dtype=jnp.int32)
    products = index_values[:, None] * index_values[None, :] % length
    angles = products.astype(jnp.float32) * (2.0 * math.pi / length)
    return jnp.cos(angles) + jnp.sin(angles)


def squared_waves(start, count, length):
    index_values = start + jnp.arange(count, dtype=jnp.int32)
    signed = jnp.where(index_values < length // 2, index_values, index_values - length)
    waves = signed.astype(jnp.float32) * (2.0 * math.pi / length)
    return waves * waves


def general(orbitals, sources):
    band_count, slab_x, full_y, full_z = orbitals.shape
    grid_count = lax.axis_size("grid")
    full_x = slab_x * grid_count
    total_bands = band_count * lax.axis_size("band")
    round_count = sources.shape[0]
    table_x = cas_table(full_x)
    table_y = cas_table(full_y)
    table_z = cas_table(full_z)
    column_y = full_y // grid_count
    start_y = lax.axis_index("grid") * column_y
    waves = (
        squared_waves(0, full_x, full_x)[:, None, None]
        + squared_waves(start_y, column_y, full_y)[None, :, None]
        + squared_waves(0, full_z, full_z)[None, None, :]
    )
    screen = (4.0 * math.pi / full_x) ** 2
    volume = 1.0 / (full_x * full_y * full_z)
    kernel = volume / (waves + screen)

    def plane_transform(field):
        spread = jnp.einsum("bxyz,zk->bxyk", field, table_z, precision=highest)
        return jnp.einsum("bxyk,yj->bxjk", spread, table_y, precision=highest)

    def own_slab(number):
        owner = number // band_count
        local = number % band_count
        return (owner, lax.dynamic_index_in_dim(orbitals, local, 0, keepdims=False))

    def fetch(number):
        owner, slab = own_slab(number)
        return spread_2(slab, "band", owner)

    arrived = [fetch(sources[turn]) for turn in range(round_count)]
    terms = jnp.zeros(orbitals.shape, jnp.float32)
    for turn in range(round_count):
        source = arrived[turn][None]
        spectra = plane_transform(orbitals * source)
        potential_columns = lax.all_to_all(spectra, "grid", split_axis=2, concat_axis=1, tiled=True)
        line_spread = jnp.einsum("bxyz,xa->bayz", potential_columns, table_x, precision=highest)
        line_spread = line_spread * kernel[None]
        filtered = jnp.einsum("bayz,ax->bxyz", line_spread, table_x, precision=highest)
        terms = terms + source * plane_transform(
            lax.all_to_all(filtered, "grid", split_axis=1, concat_axis=2, tiled=True)
        )
    orbital_cols, term_cols = (
        lax.all_to_all(orbitals, "band", split_axis=2, concat_axis=0, tiled=True),
        lax.all_to_all(terms, "band", split_axis=2, concat_axis=0, tiled=True),
    )
    flat_orbitals = orbital_cols.reshape(total_bands, -1)
    flat_terms = term_cols.reshape(total_bands, -1)
    partial_intersection = (
        jnp.dot(flat_orbitals, flat_terms.T, precision=highest, preferred_element_type=jnp.float32)
        * volume
    )
    intersection = lax.psum(partial_intersection, ("band", "grid"))
    factor = jnp.linalg.cholesky(intersection)
    solved = lax.linalg.triangular_solve(factor, flat_terms, left_side=True, lower=True)
    return (-solved).reshape(term_cols.shape)


def parts_of(value):
    high = value.astype(jnp.bfloat16)
    low = (value - high.astype(jnp.float32)).astype(jnp.bfloat16)
    return high, low


def along_rows(left, first, second):
    n = first.shape[0]
    h0, l0 = parts_of(first)
    h1, l1 = parts_of(second)
    right = jnp.concatenate(
        [jnp.concatenate([h0, h1], axis=1), jnp.concatenate([l0, l1], axis=1)], axis=0
    )
    both = jnp.dot(left, right, preferred_element_type=jnp.float32)
    return both[:n] + both[n:]


def along_lanes(rows, right):
    n = rows.shape[1]
    high, low = parts_of(rows)
    both = jnp.dot(
        jnp.concatenate([high, low], axis=1), right, preferred_element_type=jnp.float32
    )
    return both[:, :n] + both[:, n:]


def whole_kernel(
    bands, grids, rounds, chunks, unit, ahead, n, volume,
    sources, orbitals, left_ref, right_ref, waves_ref, out, *scratch,
):
    (own, mate, up, dn, src, fcol, spec, cols, back, terms, tcol, part, sums_b, sums_g, splat,
     in_sem, m_send, m_recv, up_send, up_recv, dn_send, dn_recv, s_send, s_recv,
     o_send, o_recv, f_send, f_recv, b_send, b_recv,
     t_send, t_recv, sb_send, sb_recv, sg_send, sg_recv) = scratch
    b = lax.axis_index("band")
    g = lax.axis_index("grid")
    nz = bands // 2
    z, core = b // 2, b % 2
    slab = n // grids
    depth = slab // chunks
    ycols = n // grids
    piece = ycols * depth
    yb = n // bands
    half = slab // 2
    units = half // unit
    total_units = rounds * units
    lag = (nz - 1) * ahead
    partner = z * 2 + (1 - core)

    barrier = pltpu.get_barrier_semaphore()
    for d in range(1, bands):
        pl.semaphore_signal(barrier, inc=1, device_id=(lax.rem(b + d, bands), g), device_id_type=MESH)
    for d in range(1, grids):
        pl.semaphore_signal(barrier, inc=1, device_id=(b, lax.rem(g + d, grids)), device_id_type=MESH)
    loads = [
        pltpu.make_async_copy(
            orbitals.at[0, pl.ds(h * half, half)], own.at[pl.ds(h * half, half)], in_sem.at[h]
        )
        for h in range(2)
    ]
    for load in loads:
        load.start()
    for load in loads:
        load.wait()
    pl.semaphore_wait(barrier, bands + grids - 2)

    def mate_copy(u):
        return pltpu.make_async_remote_copy(
            src_ref=own.at[pl.ds((1 - core) * half + u * unit, unit)],
            dst_ref=mate.at[pl.ds(u * unit, unit)],
            send_sem=m_send.at[u], recv_sem=m_recv.at[u],
            device_id=(partner, g), device_id_type=MESH,
        )

    def up_copy(v):
        return pltpu.make_async_remote_copy(
            src_ref=up.at[v], dst_ref=up.at[v],
            send_sem=up_send.at[v], recv_sem=up_recv.at[v],
            device_id=(lax.rem(b + 2, bands), g), device_id_type=MESH,
        )

    def dn_copy(v):
        return pltpu.make_async_remote_copy(
            src_ref=dn.at[v], dst_ref=dn.at[v],
            send_sem=dn_send.at[v], recv_sem=dn_recv.at[v],
            device_id=(lax.rem(b + bands - 2, bands), g), device_id_type=MESH,
        )

    def src_copy(v, side):
        r, u = lax.div(v, units), lax.rem(v, units)
        block = src.at[r, pl.ds(side * half + u * unit, unit)]
        return pltpu.make_async_remote_copy(
            src_ref=block, dst_ref=block,
            send_sem=s_send.at[v], recv_sem=s_recv.at[v],
            device_id=(partner, g), device_id_type=MESH,
        )

    for u in range(units):
        mate_copy(u).start()

    def step(t, _):
        @pl.when(t < units)
        def _():
            mate_copy(t).wait_recv()

        def pass_on(v, box, copy, first, last):
            @pl.when(jnp.logical_and(v >= 0, v < total_units))
            def _():
                r, u = lax.div(v, units), lax.rem(v, units)
                s = sources[r]
                here = jnp.where(
                    s == b, own[pl.ds(core * half + u * unit, unit)], mate[pl.ds(u * unit, unit)]
                )

                @pl.when(first)
                def _():
                    box[v] = here

                @pl.when(jnp.logical_not(first))
                def _():
                    copy(v).wait_recv()
                    box[v] = jnp.where(jnp.logical_or(s == b, s == partner), here, box[v])

                @pl.when(jnp.logical_not(last))
                def _():
                    copy(v).start()

        pass_on(t - z * ahead, up, up_copy, z == 0, z == nz - 1)
        pass_on(t - (nz - 1 - z) * ahead, dn, dn_copy, z == nz - 1, z == 0)
        v = t - lag

        @pl.when(v >= 0)
        def _():
            r, u = lax.div(v, units), lax.rem(v, units)
            src[r, pl.ds(core * half + u * unit, unit)] = jnp.where(
                sources[r] < 2 * z + 2, up[v], dn[v]
            )
            src_copy(v, core).start()

        return 0

    def o_copy(target, owner):
        return pltpu.make_async_remote_copy(
            src_ref=own.at[:, pl.ds(target * yb, yb)], dst_ref=fcol.at[owner],
            send_sem=o_send.at[target], recv_sem=o_recv.at[owner],
            device_id=(target, g), device_id_type=MESH,
        )

    left = left_ref[...]
    right = right_ref[...]

    def f_copy(c, r, target, owner):
        return pltpu.make_async_remote_copy(
            src_ref=spec.at[c * rounds + r, pl.ds(target * piece, piece)],
            dst_ref=cols.at[r, owner * chunks + c],
            send_sem=f_send.at[(c * rounds + r) * grids + target],
            recv_sem=f_recv.at[(c * rounds + r) * grids + owner],
            device_id=(b, target), device_id_type=MESH,
        )

    def b_copy(c, r, target, owner):
        return pltpu.make_async_remote_copy(
            src_ref=cols.at[r, target * chunks + c],
            dst_ref=back.at[c * rounds + r, pl.ds(owner * piece, piece)],
            send_sem=b_send.at[(c * rounds + r) * grids + target],
            recv_sem=b_recv.at[(c * rounds + r) * grids + owner],
            device_id=(b, target), device_id_type=MESH,
        )

    base = waves_ref[...]
    chunk_units = depth // unit

    def forward_chunk(c, r):
        for k in range(0, depth, 2):
            at = c * depth + k
            pair = src[r, pl.ds(at, 2)] * own[pl.ds(at, 2)]
            rows = along_lanes(pair.reshape(2 * n, n), right)
            planes = along_rows(left, rows[:n], rows[n:])
            spec[c * rounds + r, pl.ds(k, n, stride=depth), :] = planes[:, :n]
            spec[c * rounds + r, pl.ds(k + 1, n, stride=depth), :] = planes[:, n:]
        for d in range(1, grids):
            f_copy(c, r, lax.rem(g + d, grids), g).start()
        cols[r, g * chunks + c] = spec[c * rounds + r, pl.ds(g * piece, piece), :]

    def forward(r):
        def phase(i, _):
            start = r * units + i * chunk_units + lag
            if r == 0:
                lax.fori_loop(jnp.where(i == 0, 0, start), start + chunk_units, step, 0)
            else:
                lax.fori_loop(start, start + chunk_units, step, 0)

            def side(e, _):
                @pl.when(e == 1)
                def _():
                    for u in range(chunk_units):
                        src_copy(r * units + i * chunk_units + u, 1 - core).wait_recv()

                where = jnp.where(e == 0, core, 1 - core)
                forward_chunk(where * (chunks // 2) + i, r)
                return 0

            lax.fori_loop(0, 2, side, 0)
            return 0

        lax.fori_loop(0, chunks // 2, phase, 0)

    def lines(r):
        for c in range(chunks):
            for d in range(1, grids):
                f_copy(c, r, g, lax.rem(g + d, grids)).wait_recv()

        def line(k, _):
            held = [
                cols[r, :, pl.ds(pl.multiple_of((2 * k + e) * depth, depth), depth), :].reshape(n, n)
                for e in range(2)
            ]
            moved = along_rows(left, held[0], held[1])
            filtered = []
            for e in range(2):
                ky = g * ycols + 2 * k + e
                signed = jnp.where(ky < n // 2, ky, ky - n).astype(jnp.float32)
                wave = signed * (2.0 * math.pi / n)
                filtered.append(moved[:, e * n:(e + 1) * n] * (volume / (base + wave * wave)))
            done = along_rows(left, filtered[0], filtered[1])
            for e in range(2):
                cols[r, :, pl.ds(pl.multiple_of((2 * k + e) * depth, depth), depth), :] = (
                    done[:, e * n:(e + 1) * n].reshape(grids * chunks, depth, n)
                )
            return 0

        lax.fori_loop(0, ycols // 2, line, 0)

    def give_back(c, r):
        for d in range(1, grids):
            b_copy(c, r, lax.rem(g + d, grids), g).start()

    def inverse(c, r):
        for d in range(1, grids):
            b_copy(c, r, g, lax.rem(g + d, grids)).wait_recv()
        back[c * rounds + r, pl.ds(g * piece, piece), :] = cols[r, g * chunks + c]
        for k in range(0, depth, 2):
            planes = along_rows(
                left,
                back[c * rounds + r, pl.ds(k, n, stride=depth), :],
                back[c * rounds + r, pl.ds(k + 1, n, stride=depth), :],
            )
            rows = jnp.concatenate([planes[:, :n], planes[:, n:]], axis=0)
            potential = along_lanes(rows, right).reshape(2, n, n)
            at = c * depth + k
            here = src[r, pl.ds(at, 2)] * potential
            if r == 0:
                terms[pl.ds(at, 2)] = here
            else:
                terms[pl.ds(at, 2)] += here

    def inverse_all(r):
        def one(c, _):
            inverse(c, r)
            return 0

        lax.fori_loop(0, chunks, one, 0)

    tail = min(2, rounds)
    returned = 0
    for r in range(rounds):
        forward(r)
        if r == rounds - 1:
            for d in range(1, bands):
                o_copy(lax.rem(b + d, bands), b).start()
        if r % 2 == 1 and returned < rounds - tail:
            lines(returned)
            for c in range(chunks):
                give_back(c, returned)
            returned += 1
            ready = returned - 1
            if ready > 0:
                inverse_all(ready - 1)
    while returned < rounds - tail:
        lines(returned)
        for c in range(chunks):
            give_back(c, returned)
        returned += 1
        if returned > 1:
            inverse_all(returned - 2)
    for r in range(rounds - tail, rounds):
        lines(r)
    for c in range(chunks):
        for r in range(rounds - tail, rounds):
            give_back(c, r)
    fcol[b] = own[:, pl.ds(b * yb, yb), :]
    if rounds > tail:
        inverse_all(rounds - tail - 1)

    def t_copy(c, target, owner):
        return pltpu.make_async_remote_copy(
            src_ref=terms.at[pl.ds(c * depth, depth), pl.ds(target * yb, yb)],
            dst_ref=tcol.at[owner, pl.ds(c * depth, depth)],
            send_sem=t_send.at[c * bands + target],
            recv_sem=t_recv.at[c * bands + owner],
            device_id=(target, g), device_id_type=MESH,
        )

    def overlap(c):
        for d in range(1, bands):
            t_copy(c, b, lax.rem(b + d, bands)).wait_recv()

        def one(i, _):
            mine = fcol[i, pl.ds(c * depth, depth)]
            for k in range(bands):
                prod = mine * tcol[k, pl.ds(c * depth, depth)]
                total = jnp.sum(prod.reshape(-1, 8, n), axis=0)
                if c == 0:
                    part[i * bands + k] = total
                else:
                    part[i * bands + k] += total
            return 0

        lax.fori_loop(0, bands, one, 0)

    for c in range(chunks):
        for r in range(rounds - tail, rounds):
            inverse(c, r)
        for d in range(1, bands):
            t_copy(c, lax.rem(b + d, bands), b).start()
        tcol[b, pl.ds(c * depth, depth)] = terms[pl.ds(c * depth, depth), pl.ds(b * yb, yb), :]
        if c == 1:
            for d in range(1, bands):
                o_copy(b, lax.rem(b + d, bands)).wait_recv()
        if c > 0:
            overlap(c - 1)
    overlap(chunks - 1)

    count = bands * bands
    flat = jnp.sum(part[...], axis=1)
    if count < n:
        flat = jnp.concatenate([flat, jnp.zeros((n - count, n), jnp.float32)], axis=0)
    lanes = jnp.sum(flat.T, axis=0, keepdims=True)
    sums_b[b] = jnp.broadcast_to(lanes, (8, n))

    def sb_copy(target, owner):
        return pltpu.make_async_remote_copy(
            src_ref=sums_b.at[b], dst_ref=sums_b.at[owner],
            send_sem=sb_send.at[target], recv_sem=sb_recv.at[owner],
            device_id=(target, g), device_id_type=MESH,
        )

    def sg_copy(target, owner):
        return pltpu.make_async_remote_copy(
            src_ref=sums_g.at[g], dst_ref=sums_g.at[owner],
            send_sem=sg_send.at[target], recv_sem=sg_recv.at[owner],
            device_id=(b, target), device_id_type=MESH,
        )

    for d in range(1, bands):
        sb_copy(lax.rem(b + d, bands), b).start()
    for d in range(1, bands):
        sb_copy(b, lax.rem(b + d, bands)).wait_recv()
    sums_g[g] = jnp.sum(sums_b[...], axis=0)
    for d in range(1, grids):
        sg_copy(lax.rem(g + d, grids), g).start()
    for d in range(1, grids):
        sg_copy(g, lax.rem(g + d, grids)).wait_recv()
    total = jnp.sum(sums_g[...], axis=0)[:1] * volume
    splat[...] = jnp.broadcast_to(total, (n, n)).T

    def entry(i, k):
        first = splat[pl.ds(i * bands + k, 1), :]
        return 0.5 * (first + splat[pl.ds(k * bands + i, 1), :])

    factor = {}
    inverse_diag = {}
    for k in range(bands):
        diag = entry(k, k)
        for m in range(k):
            diag = diag - factor[k, m] * factor[k, m]
        inverse_diag[k] = 1.0 / jnp.sqrt(diag)
        for i in range(k + 1, bands):
            value = entry(i, k)
            for m in range(k):
                value = value - factor[i, m] * factor[k, m]
            factor[i, k] = value * inverse_diag[k]
    for k in range(bands):
        splat[pl.ds(k * bands + k, 1), :] = inverse_diag[k]
        for i in range(k + 1, bands):
            splat[pl.ds(i * bands + k, 1), :] = factor[i, k]

    def solve(x, _):
        solved = []
        for i in range(bands):
            value = -tcol[i, x]
            for k in range(i):
                value = value - splat[pl.ds(i * bands + k, 1), :] * solved[k]
            value = value * splat[pl.ds(i * bands + i, 1), :]
            out[i, x] = value
            solved.append(value)
        return 0

    lax.fori_loop(0, slab, solve, 0)

    for u in range(units):
        mate_copy(u).wait_send()

    def settle(v, _):
        @pl.when(z < nz - 1)
        def _():
            up_copy(v).wait_send()

        @pl.when(z > 0)
        def _():
            dn_copy(v).wait_send()

        src_copy(v, core).wait_send()
        return 0

    lax.fori_loop(0, total_units, settle, 0)
    for d in range(1, bands):
        o_copy(lax.rem(b + d, bands), b).wait_send()
    for c in range(chunks):
        for r in range(rounds):
            for d in range(1, grids):
                f_copy(c, r, lax.rem(g + d, grids), g).wait_send()
                b_copy(c, r, lax.rem(g + d, grids), g).wait_send()
        for d in range(1, bands):
            t_copy(c, lax.rem(b + d, bands), b).wait_send()
    for d in range(1, bands):
        sb_copy(lax.rem(b + d, bands), b).wait_send()
    for d in range(1, grids):
        sg_copy(lax.rem(g + d, grids), g).wait_send()


def fused(bands, grids, orbitals, sources):
    n = orbitals.shape[2]
    rounds = sources.shape[0]
    slab = n // grids
    depth = 8
    chunks = slab // depth
    yb = n // bands
    numbers = np.arange(n)
    angles = (numbers[:, None] * numbers[None, :] % n) * (2.0 * math.pi / n)
    table = jnp.asarray(np.cos(angles) + np.sin(angles), jnp.float32)
    high, low = parts_of(table)
    left = jnp.block([[high, high], [low, low]])
    right = jnp.block([[high, low], [high, low]])
    signed = np.where(numbers < n // 2, numbers, numbers - n) * (2.0 * math.pi / n)
    screen = (4.0 * math.pi / n) ** 2
    waves = jnp.asarray(signed[:, None] ** 2 + signed[None, :] ** 2 + screen, jnp.float32)
    volume = 1.0 / n**3
    f32 = jnp.float32
    dma = pltpu.SemaphoreType.DMA
    unit = 2
    units = slab // 2 // unit
    relay = rounds * units
    scratch = [
        pltpu.VMEM((slab, n, n), f32),
        pltpu.VMEM((slab // 2, n, n), f32),
        pltpu.VMEM((relay, unit, n, n), f32),
        pltpu.VMEM((relay, unit, n, n), f32),
        pltpu.VMEM((rounds, slab, n, n), f32),
        pltpu.VMEM((bands, slab, yb, n), f32),
        pltpu.VMEM((chunks * rounds, n * depth, n), f32),
        pltpu.VMEM((rounds, grids * chunks, (n // grids) * depth, n), f32),
        pltpu.VMEM((chunks * rounds, n * depth, n), f32),
        pltpu.VMEM((slab, n, n), f32),
        pltpu.VMEM((bands, slab, yb, n), f32),
        pltpu.VMEM((bands * bands, 8, n), f32),
        pltpu.VMEM((bands, 8, n), f32),
        pltpu.VMEM((grids, 8, n), f32),
        pltpu.VMEM((n, n), f32),
        dma((2,)),
        dma((units,)),
        dma((units,)),
        dma((relay,)),
        dma((relay,)),
        dma((relay,)),
        dma((relay,)),
        dma((relay,)),
        dma((relay,)),
        dma((bands,)),
        dma((bands,)),
        dma((chunks * rounds * grids,)),
        dma((chunks * rounds * grids,)),
        dma((chunks * rounds * grids,)),
        dma((chunks * rounds * grids,)),
        dma((chunks * bands,)),
        dma((chunks * bands,)),
        dma((bands,)),
        dma((bands,)),
        dma((grids,)),
        dma((grids,)),
    ]
    vmem = pl.BlockSpec(memory_space=pltpu.VMEM)
    return pl.pallas_call(
        functools.partial(whole_kernel, bands, grids, rounds, chunks, unit, 2, n, volume),
        out_shape=jax.ShapeDtypeStruct((bands, slab, yb, n), f32),
        in_specs=[
            pl.BlockSpec(memory_space=pltpu.SMEM),
            pl.BlockSpec(memory_space=pl.ANY),
            vmem, vmem, vmem,
        ],
        out_specs=vmem,
        scratch_shapes=scratch,
        compiler_params=pltpu.CompilerParams(
            collective_id=0, has_side_effects=True, vmem_limit_bytes=60 * 1024 * 1024
        ),
        name="exchange",
    )(sources, orbitals, left, right, waves)


def per_device(orbitals, sources):
    held, slab, full_y, full_z = orbitals.shape
    bands = lax.axis_size("band")
    grids = lax.axis_size("grid")
    n = full_y
    fits = (
        held == 1 and n == full_z == slab * grids and n % 128 == 0 and slab % 16 == 0
        and bands % 2 == 0 and bands * bands <= n and n % (8 * bands) == 0
        and 4 * n * n * slab * (5 * sources.shape[0] + 6) <= 54 * 2**20
    )
    if fits:
        return fused(bands, grids, orbitals, sources)
    return general(orbitals, sources)


def solution(mesh):
    placed = (P("band", "grid", None, None), P())
    return jax.shard_map(
        per_device,
        mesh=mesh,
        in_specs=placed,
        out_specs=P(None, "grid", "band", None),
        check_vma=False,
    )
```
